512 devices in a mesh: gx: 16 (over z), gy: 4 (over x), gz: 8 (over y, core).
Axes of the slice: x: 4, y: 4, z: 16, core: 2. Of those that a mesh axis runs over, the one named last changes fastest.
Arguments:
- density: float32 [512, 64, 1024], P('gx', 'gy', 'gz'), may hold values from 0.5 to 2
- momentum: float32 [2, 512, 64, 1024], P(None, 'gx', 'gy', 'gz'), may hold values from -3 to 3
- lower_face: float32 [512], P('gx'), may hold values from 2048 to 8192
Outputs:
- updated: float32 [3, 512, 64, 1024], P(None, 'gx', 'gy', 'gz')
The draws below stay inside these ranges and needn't reach their ends.
All inputs are finite; a program needn't handle non-finite values.
Results may differ from the reference program's by a relative error of at most 0.0003.
Values sent between devices are 32-bit elements; how exact they have to be, the bound alone decides.
A program may use at most 64 MiB of HBM per device.

```python
import math
import jax
import jax.numpy as jnp
from jax import lax

NX = 512
NY = 64
NZ = 1024


def steps_of(own_key, extent, shards, low, largest):
    def one(axis_at, blocks):
        heights = jax.random.uniform(jax.random.fold_in(jax.random.fold_in(own_key, 6), axis_at), (blocks,), jnp.float32, low / len(shards), largest / len(shards))
        return jnp.repeat(jnp.exp(heights), extent[axis_at] // blocks).reshape((-1,) + (1,) * (len(extent) - axis_at - 1))

    factor_of = one(*shards[0])
    for cut in shards[1:]:
        factor_of = factor_of * one(*cut)
    return factor_of


def gaussian(stream_key, dims, width, limit, shards=(), kind=jnp.bfloat16):
    array = jax.random.normal(stream_key, dims, jnp.float32) * width
    if len(shards) > 0:
        array = steps_of(stream_key, dims, shards, -0.22, 0.18) * array
    return jnp.clip(array, min=-limit, max=limit).astype(kind)


def setup_inputs(seed: int = 0) -> dict:
    arg_keys = jax.random.split(jax.random.key(seed), 4)
    density = jnp.clip(0.5 + 1.5 * jax.random.uniform(arg_keys[0], (NX, NY, NZ), jnp.float32) ** steps_of(arg_keys[0], (NX, NY, NZ), ((0, 16), (1, 4), (2, 8)), -0.2, 0.2), 0.5, 2.0)
    momentum = gaussian(arg_keys[1], (2, NX, NY, NZ), 0.5, 3.0, ((1, 16), (2, 4), (3, 8)), jnp.float32)
    lower_face = jnp.clip(jnp.exp(math.log(8192.0) - 1.3862944 * jax.random.uniform(arg_keys[2], (NX,), jnp.float32) ** steps_of(arg_keys[2], (NX,), ((0, 16),), -0.2, 0.2)), 2048.0, 8192.0)
    return dict(density=density, momentum=momentum, lower_face=lower_face)


time_step = 0.2


def central_sixth(field, axis):
    def diff(k):
        return jnp.roll(field, -k, axis) - jnp.roll(field, k, axis)
    return (45.0 * diff(1) - 9.0 * diff(2) + diff(3)) / 60.0


def reference(density, momentum, lower_face):
    state = jnp.concatenate([density[None], momentum], 0)
    flux_y = state * (state[1] / state[0])[None]
    flux_z = state * (state[2] / state[0])[None]
    rhs = state - time_step * (central_sixth(flux_y, 2) + central_sixth(flux_z, 3))
    upper = jnp.concatenate([lower_face[1:], lower_face[-1:]])
    diagonal = 1.0 + lower_face + upper
    position = jnp.arange(lower_face.shape[0], dtype=jnp.int32)
    below = jnp.where(position == 0, jnp.zeros_like(lower_face), -lower_face)
    above = -upper

    def coef_step(carry, items):
        sub, dia, sup = items
        denom = dia - sub * carry
        value = sup / denom
        return value, (value, denom)

    start = jnp.zeros((), jnp.float32)
    _, (primes, denoms) = lax.scan(coef_step, start, (below, diagonal, above))
    moved = jnp.moveaxis(rhs, 1, 0)

    def fwd_step(carry, items):
        sub, denom, row = items
        value = (row - sub * carry) / denom
        return value, value

    zero_row = jnp.zeros(moved.shape[1:], jnp.float32)
    _, dprime = lax.scan(fwd_step, zero_row, (below, denoms, moved))

    def back_step(carry, items):
        prime, row = items
        value = row - prime * carry
        return value, value

    _, solved = lax.scan(back_step, zero_row, (primes, dprime), reverse=True)
    return jnp.moveaxis(solved, 0, 1)
```

```python
import functools

import jax
import jax.numpy as jnp
from jax import lax
from jax.experimental import pallas as pl
from jax.experimental.pallas import tpu as pltpu
from jax.sharding import PartitionSpec as P

MESH = pl.DeviceIdType.MESH
ANY = pl.BlockSpec(memory_space=pl.ANY)
VMEM = pl.BlockSpec(memory_space=pltpu.VMEM)
LANES = 128
WEIGHTS = (45.0, -9.0, 1.0)
SCALE = 0.2 / 60.0
NEAR = 4


def neighbour(axis, count, offset):
    return {axis: lax.rem(lax.axis_index(axis) + (offset + count), count)}


def stencil_matrix():
    source = lax.broadcasted_iota(jnp.int32, (2 * LANES, LANES), 0)
    target = lax.broadcasted_iota(jnp.int32, (2 * LANES, LANES), 1)
    own = source < LANES
    offset = jnp.where(own, source, source - LANES) - target
    matrix = jnp.zeros((2 * LANES, LANES), jnp.float32)
    for step, weight in enumerate(WEIGHTS, 1):
        for sign in (1, -1):
            inner = own & (offset == sign * step)
            wrapped = (source >= LANES) & (offset == sign * (step - LANES))
            matrix = jnp.where(inner | wrapped, sign * weight, matrix)
    return matrix.astype(jnp.bfloat16)


def along_z(own, halo, matrix):
    both = jnp.concatenate([own, halo], axis=1)
    high = both.astype(jnp.bfloat16)
    rest = both - high.astype(jnp.float32)
    middle = rest.astype(jnp.bfloat16)
    low = (rest - middle.astype(jnp.float32)).astype(jnp.bfloat16)
    dot = functools.partial(jnp.dot, preferred_element_type=jnp.float32)
    return dot(high, matrix) + (dot(middle, matrix) + dot(low, matrix))


def along_y(rows_at):
    total = None
    for step, weight in enumerate(WEIGHTS, 1):
        term = weight * (rows_at(step) - rows_at(-step))
        total = term if total is None else total + term
    return total


def pack_lanes(tiles):
    slot = lax.broadcasted_iota(jnp.int32, (8, LANES), 1) // 6
    packed = jnp.zeros((8, LANES), jnp.float32)
    for k, tile in enumerate(tiles):
        packed = jnp.where(slot == k, pltpu.roll(tile, 6 * k + 3, 1), packed)
    return packed


def unpack_lanes(from_left, from_right, count):
    lane = lax.broadcasted_iota(jnp.int32, (8, LANES), 1)
    both = jnp.where(lax.rem(lane, 6) < 3, from_left, from_right)
    return [pltpu.roll(both, (125 - 6 * k) % LANES, 1) for k in range(count)]


def tiles_of(planes):
    return [plane[8 * h : 8 * h + 8] for plane in planes for h in range(2)]


def solve_kernel(
    counts,
    density,
    momentum,
    face,
    local_out,
    phi_out,
    ends_out,
    face_s,
    state,
    flux_y,
    flux_zz,
    reduced_y,
    z_pack,
    z_left,
    z_right,
    send_a,
    recv_a,
    send_b,
    recv_b,
    coef,
    matrix_s,
    local,
    phi,
    in_sem,
    halo_send,
    halo_recv,
    a_send,
    a_recv,
    b_send,
    b_recv,
    out_sem,
    far_sem,
):
    nx, ny, nz = counts
    cells = state.shape[1]
    me = lax.axis_index("gx")

    barrier = pltpu.get_barrier_semaphore()
    near = [("gx", nx, k) for step in range(1, NEAR + 1) for k in (step, -step)]
    near += [("gy", ny, 1), ("gy", ny, -1), ("gz", nz, 1), ("gz", nz, -1)]
    for axis, count, offset in near:
        pl.semaphore_signal(
            barrier, inc=1, device_id=neighbour(axis, count, offset), device_id_type=MESH
        )
    loads = [
        pltpu.make_async_copy(face, face_s, in_sem.at[0]),
        pltpu.make_async_copy(density, state.at[0], in_sem.at[1]),
        pltpu.make_async_copy(momentum.at[0], state.at[1], in_sem.at[2]),
        pltpu.make_async_copy(momentum.at[1], state.at[2], in_sem.at[3]),
    ]
    for load in loads:
        load.start()
    matrix_s[...] = stencil_matrix()
    zero_rows = jnp.zeros((16, LANES), jnp.float32)
    send_b[pl.ds(6, 16, stride=8), :] = zero_rows
    send_b[pl.ds(7, 16, stride=8), :] = zero_rows
    for load in loads:
        load.wait()

    def inverse_face(i):
        return 1.0 / jnp.full((8, LANES), face_s[i], jnp.float32)

    def reduce_step(i, carry):
        pairs, base = carry
        inv = inverse_face(i)
        inv_rows = jnp.concatenate([inv, inv], 0)
        base = [(u + g * inv, g) for u, g in base]
        phi[0, i] = base[0][0]
        phi[1, i] = base[1][0]
        base = [(u, g + u) for u, g in base]
        rho, m0, m1 = state[0, i], state[1, i], state[2, i]
        over = 1.0 / rho
        speed_y = m0 * over
        speed_z = m1 * over
        yy, yz, zz = m0 * speed_y, m1 * speed_y, m1 * speed_z
        flux_y[0, i, 8:24] = m0
        flux_y[1, i, 8:24] = yy
        flux_y[2, i, 8:24] = yz
        flux_zz[i] = zz
        out = []
        for (u, g), value in zip(pairs, (rho, m0, m1, yy, yz, zz)):
            u = u + g * inv_rows
            out.append((u, g + (u - value)))
        return out, base

    def reduce_steps(block, carry):
        for k in range(4):
            carry = reduce_step(4 * block + k, carry)
        return carry

    zero = jnp.zeros((16, LANES), jnp.float32)
    unit = jnp.ones((8, LANES), jnp.float32)
    pairs, base = lax.fori_loop(
        0,
        cells // 4,
        reduce_steps,
        ([(zero, zero)] * 6, [(unit, 0.0 * unit), (0.0 * unit, unit)]),
    )
    rho_r, m0_r, m1_r, yy_r, yz_r, zz_r = pairs
    plain = [value for pair in (rho_r, m0_r, m1_r) for value in pair]
    by_y = [value for pair in (m0_r, yy_r, yz_r) for value in pair]
    by_z = [value for pair in (m1_r, yz_r, zz_r) for value in pair]
    for k in range(6):
        reduced_y[k, 8:24] = by_y[k]
    z_pack[cells // 2] = pack_lanes(tiles_of(by_z))

    pl.semaphore_wait(barrier, len(near))

    def halo(which, source, target, axis, count, offset):
        return pltpu.make_async_remote_copy(
            source,
            target,
            halo_send.at[which],
            halo_recv.at[which],
            device_id=neighbour(axis, count, offset),
            device_id_type=MESH,
        )

    last = cells // 2
    near_halos = [
        halo(0, reduced_y.at[:, 16:24], reduced_y.at[:, 0:8], "gy", ny, 1),
        halo(1, reduced_y.at[:, 8:16], reduced_y.at[:, 24:32], "gy", ny, -1),
        halo(2, z_pack.at[last], z_left.at[last], "gz", nz, 1),
        halo(3, z_pack.at[last], z_right.at[last], "gz", nz, -1),
    ]
    for copy in near_halos:
        copy.start()
    for offset in (NEAR, -NEAR):
        pl.semaphore_signal(
            far_sem, inc=1, device_id=neighbour("gx", nx, offset), device_id_type=MESH
        )
    raw_y = [
        halo(4, flux_y.at[:, :, 16:24], flux_y.at[:, :, 0:8], "gy", ny, 1),
        halo(5, flux_y.at[:, :, 8:16], flux_y.at[:, :, 24:32], "gy", ny, -1),
    ]
    for copy in raw_y:
        copy.start()

    (u1, g1), (u2, g2) = base
    low_half = lax.broadcasted_iota(jnp.int32, (8, LANES), 1) < LANES // 2
    row6 = jnp.where(low_half, u1, u2)
    row7 = jnp.where(low_half, g1, inverse_face(cells - 1))
    for h in range(2):
        send_a[pl.ds(64 * h + 6, 8, stride=8), :] = row6
        send_a[pl.ds(64 * h + 7, 8, stride=8), :] = row7

    for copy in near_halos:
        copy.wait_recv()
    own_z = jnp.concatenate(by_z, 0)
    halo_z = jnp.concatenate(unpack_lanes(z_left[last], z_right[last], 12), 0)
    diff_z = along_z(own_z, halo_z, matrix_s[...])
    for f in range(3):
        for v in range(2):
            k = 2 * f + v
            diff_y = along_y(lambda step: reduced_y[k, pl.ds(8 + step, 16), :])
            value = plain[k] - SCALE * (diff_y + diff_z[16 * k : 16 * k + 16])
            for h in range(2):
                send_a[pl.ds(64 * h + 3 * v + f, 8, stride=8), :] = value[8 * h : 8 * h + 8]

    def rows(index):
        return pl.ds(pl.multiple_of(index * 8, 8), 8)

    order = [k for step in range(nx // 2, 0, -1) for k in sorted({step, nx - step})]

    def exchange(source, target, send, recv, k):
        other = lax.rem(me + k, nx)
        return pltpu.make_async_remote_copy(
            source.at[rows(other)],
            target.at[rows(me)],
            send.at[k],
            recv.at[k],
            device_id={"gx": other},
            device_id_type=MESH,
        )

    pl.semaphore_wait(far_sem, 2)
    phase_a = [exchange(send_a, recv_a, a_send, a_recv, k) for k in order]
    for copy in phase_a:
        copy.start()
    recv_a[rows(me), :] = send_a[rows(me), :]

    def pack_step(p, _):
        planes = []
        for q in range(2):
            i = 2 * p + q
            planes += [state[2, i], flux_y[2, i, 8:24], flux_zz[i]]
        z_pack[p] = pack_lanes(tiles_of(planes))
        return _

    lax.fori_loop(0, last, pack_step, 0)
    raw_z = [
        halo(6, z_pack.at[0:last], z_left.at[0:last], "gz", nz, 1),
        halo(7, z_pack.at[0:last], z_right.at[0:last], "gz", nz, -1),
    ]
    for copy in raw_z:
        copy.start()
    for copy in raw_y + raw_z:
        copy.wait_recv()

    def local_step(p, carry):
        planes = []
        for q in range(2):
            i = 2 * p + q
            planes += [state[2, i], flux_y[2, i, 8:24], flux_zz[i]]
        halos = unpack_lanes(z_left[p], z_right[p], 12)
        diff_z = along_z(jnp.concatenate(planes, 0), jnp.concatenate(halos, 0), matrix_s[...])
        for q in range(2):
            i = 2 * p + q
            inv = inverse_face(i)
            inv_rows = jnp.concatenate([inv, inv], 0)
            new = []
            for f, (u, g) in enumerate(carry):
                diff_y = along_y(lambda step: flux_y[f, i, pl.ds(8 + step, 16), :])
                at = 16 * (3 * q + f)
                value = state[f, i] - SCALE * (diff_y + diff_z[at : at + 16])
                u = u + g * inv_rows
                local[f, i] = u
                new.append((u, g + (u - value)))
            carry = new
        return carry

    lax.fori_loop(0, last, local_step, [(zero, zero)] * 3)
    stores = [
        pltpu.make_async_copy(local, local_out, out_sem.at[0]),
        pltpu.make_async_copy(phi, phi_out, out_sem.at[1]),
    ]
    for store in stores:
        store.start()

    for copy in phase_a:
        copy.wait_recv()

    low_rows = lax.broadcasted_iota(jnp.int32, (16, LANES), 1) < LANES // 2
    row6 = recv_a[pl.ds(6, 16, stride=8), :]
    row7 = recv_a[pl.ds(7, 16, stride=8), :]
    turn6 = pltpu.roll(row6, LANES // 2, 1)
    turn7 = pltpu.roll(row7, LANES // 2, 1)
    t_uu = jnp.where(low_rows, row6, turn6)
    t_ug = jnp.where(low_rows, turn6, row6)
    t_gu = jnp.where(low_rows, row7, turn7)
    coef[0] = t_uu
    coef[1] = t_ug
    coef[2] = t_gu
    coef[3] = (1.0 + t_ug * t_gu) / t_uu
    coef[4] = jnp.where(low_rows, turn7, row7)

    def at_row(which, j):
        return jnp.broadcast_to(coef[which, pl.ds(j, 1), :], (3, LANES))

    blocks = [[at_row(which, j) for which in range(4)] for j in range(nx)]
    one = jnp.ones((3, LANES), jnp.float32)
    from_left = [(0.0 * one, one)]
    for j in range(nx):
        uu, ug, gu, gg = blocks[j]
        u, g = from_left[-1]
        from_left.append((uu * u + ug * g, gu * u + gg * g))
    from_right = [None] * nx + [(at_row(4, nx - 1), one)]
    for j in range(nx - 1, -1, -1):
        uu, ug, gu, gg = blocks[j]
        u, h = from_right[j + 1]
        from_right[j] = (gg * u + ug * h, gu * u + uu * h)
    norm = -1.0 / from_right[0][0]
    left_sums, right_terms = [0.0 * one], []
    for j in range(nx):
        u_r = recv_a[pl.ds(8 * j, 3), :]
        g_r = recv_a[pl.ds(8 * j + 3, 3), :]
        u, g = from_left[j + 1]
        left_sums.append(left_sums[-1] + (u * g_r - g * u_r))
        u, h = from_right[j + 1]
        right_terms.append(u * g_r + h * u_r)
    right_sum = 0.0 * one
    for d in range(nx - 1, -1, -1):
        right_sum = right_sum + right_terms[d]
        right, left = right_sum * norm, left_sums[d] * norm
        send_b[pl.ds(8 * d, 3), :] = right * from_left[d][0] + left * from_right[d][0]
        send_b[pl.ds(8 * d + 3, 3), :] = right * from_left[d][1] - left * from_right[d][1]

    phase_b = [exchange(send_b, recv_b, b_send, b_recv, k) for k in order]
    for copy in phase_b:
        copy.start()
    recv_b[rows(me), :] = send_b[rows(me), :]
    for copy in near_halos + raw_y + raw_z + phase_a:
        copy.wait_send()
    for store in stores:
        store.wait()
    for copy in phase_b:
        copy.wait_recv()
    for v in range(2):
        for f in range(3):
            ends_out[v, f] = recv_b[pl.ds(3 * v + f, 16, stride=8), :]
    for copy in phase_b:
        copy.wait_send()


def combine_kernel(local, phi, ends, out):
    starts = [(ends[0, f], ends[1, f]) for f in range(3)]
    for i in range(local.shape[1]):
        by_u = jnp.concatenate([phi[0, i]] * 2, 0)
        by_g = jnp.concatenate([phi[1, i]] * 2, 0)
        for f, (u, g) in enumerate(starts):
            out[f, i] = local[f, i] + (by_u * u + by_g * g)


def on_device(density, momentum, lower_face):
    counts = tuple(lax.axis_size(axis) for axis in ("gx", "gy", "gz"))
    nx = counts[0]
    cells, rows, lanes = density.shape
    block = (3, cells, rows, lanes)
    f32 = jnp.float32
    sems = pltpu.SemaphoreType.DMA
    local, phi, ends = pl.pallas_call(
        functools.partial(solve_kernel, counts),
        out_shape=(
            jax.ShapeDtypeStruct(block, f32),
            jax.ShapeDtypeStruct((2, cells, 8, lanes), f32),
            jax.ShapeDtypeStruct((2, 3, rows, lanes), f32),
        ),
        in_specs=[ANY, ANY, ANY],
        out_specs=(ANY, ANY, VMEM),
        scratch_shapes=[
            pltpu.SMEM((cells,), f32),
            pltpu.VMEM(block, f32),
            pltpu.VMEM((3, cells, 32, lanes), f32),
            pltpu.VMEM((cells, rows, lanes), f32),
            pltpu.VMEM((6, 32, lanes), f32),
            pltpu.VMEM((cells // 2 + 1, 8, lanes), f32),
            pltpu.VMEM((cells // 2 + 1, 8, lanes), f32),
            pltpu.VMEM((cells // 2 + 1, 8, lanes), f32),
            pltpu.VMEM((nx * 8, lanes), f32),
            pltpu.VMEM((nx * 8, lanes), f32),
            pltpu.VMEM((nx * 8, lanes), f32),
            pltpu.VMEM((nx * 8, lanes), f32),
            pltpu.VMEM((5, nx, lanes), f32),
            pltpu.VMEM((2 * lanes, lanes), jnp.bfloat16),
            pltpu.VMEM(block, f32),
            pltpu.VMEM((2, cells, 8, lanes), f32),
            sems((4,)),
            sems((8,)),
            sems((8,)),
            sems((nx,)),
            sems((nx,)),
            sems((nx,)),
            sems((nx,)),
            sems((2,)),
            pltpu.SemaphoreType.REGULAR,
        ],
        compiler_params=pltpu.CompilerParams(collective_id=0, has_side_effects=True),
        name="solve",
    )(density, momentum, lower_face)
    return pl.pallas_call(
        combine_kernel,
        out_shape=jax.ShapeDtypeStruct(block, f32),
        in_specs=[VMEM, VMEM, VMEM],
        out_specs=VMEM,
        name="combine",
    )(local, phi, ends)


def solution(mesh):
    placed = (P("gx", "gy", "gz"), P(None, "gx", "gy", "gz"), P("gx"))
    return jax.shard_map(
        on_device, mesh=mesh, in_specs=placed, out_specs=P(None, "gx", "gy", "gz"), check_vma=False
    )
```

```python
import functools

import jax
import jax.numpy as jnp
from jax import lax
from jax.experimental import pallas as pl
from jax.experimental.pallas import tpu as pltpu
from jax.sharding import PartitionSpec as P

MESH = pl.DeviceIdType.MESH
ANY = pl.BlockSpec(memory_space=pl.ANY)
VMEM = pl.BlockSpec(memory_space=pltpu.VMEM)
HBM = pl.BlockSpec(memory_space=pltpu.HBM)
LANES = 128
WEIGHTS = (45.0, -9.0, 1.0)
SCALE = 0.2 / 60.0
NEAR = 4


def neighbour(axis, count, offset):
    return {axis: lax.rem(lax.axis_index(axis) + (offset + count), count)}


def stencil_matrix():
    source = lax.broadcasted_iota(jnp.int32, (2 * LANES, LANES), 0)
    target = lax.broadcasted_iota(jnp.int32, (2 * LANES, LANES), 1)
    own = source < LANES
    offset = jnp.where(own, source, source - LANES) - target
    matrix = jnp.zeros((2 * LANES, LANES), jnp.float32)
    for step, weight in enumerate(WEIGHTS, 1):
        for sign in (1, -1):
            inner = own & (offset == sign * step)
            wrapped = (source >= LANES) & (offset == sign * (step - LANES))
            matrix = jnp.where(inner | wrapped, sign * weight, matrix)
    return matrix.astype(jnp.bfloat16)


def along_z(own, halo, matrix):
    both = jnp.concatenate([own, halo], axis=1)
    high = both.astype(jnp.bfloat16)
    rest = both - high.astype(jnp.float32)
    middle = rest.astype(jnp.bfloat16)
    low = (rest - middle.astype(jnp.float32)).astype(jnp.bfloat16)
    dot = functools.partial(jnp.dot, preferred_element_type=jnp.float32)
    return dot(high, matrix) + (dot(middle, matrix) + dot(low, matrix))


def along_y(rows_at):
    total = None
    for step, weight in enumerate(WEIGHTS, 1):
        term = weight * (rows_at(step) - rows_at(-step))
        total = term if total is None else total + term
    return total


def pack_lanes(tiles):
    slot = lax.broadcasted_iota(jnp.int32, (8, LANES), 1) // 6
    packed = jnp.zeros((8, LANES), jnp.float32)
    for k, tile in enumerate(tiles):
        packed = jnp.where(slot == k, pltpu.roll(tile, 6 * k + 3, 1), packed)
    return packed


def unpack_lanes(from_left, from_right, count):
    lane = lax.broadcasted_iota(jnp.int32, (8, LANES), 1)
    both = jnp.where(lax.rem(lane, 6) < 3, from_left, from_right)
    return [pltpu.roll(both, (125 - 6 * k) % LANES, 1) for k in range(count)]


def tiles_of(planes):
    return [plane[8 * h : 8 * h + 8] for plane in planes for h in range(2)]


def solve_kernel(
    counts,
    density,
    momentum,
    face,
    local_out,
    phi_out,
    ends_out,
    face_s,
    state,
    flux_y,
    flux_zz,
    reduced_y,
    z_pack,
    z_left,
    z_right,
    send_a,
    recv_a,
    send_b,
    recv_b,
    coef,
    matrix_s,
    local,
    phi,
    in_sem,
    halo_send,
    halo_recv,
    a_send,
    a_recv,
    b_send,
    b_recv,
    out_sem,
    far_sem,
):
    nx, ny, nz = counts
    cells = state.shape[1]
    me = lax.axis_index("gx")

    barrier = pltpu.get_barrier_semaphore()
    near = [("gx", nx, k) for step in range(1, NEAR + 1) for k in (step, -step)]
    near += [("gy", ny, 1), ("gy", ny, -1), ("gz", nz, 1), ("gz", nz, -1)]
    for axis, count, offset in near:
        pl.semaphore_signal(
            barrier, inc=1, device_id=neighbour(axis, count, offset), device_id_type=MESH
        )
    loads = [
        pltpu.make_async_copy(face, face_s, in_sem.at[0]),
        pltpu.make_async_copy(density, state.at[0], in_sem.at[1]),
        pltpu.make_async_copy(momentum.at[0], state.at[1], in_sem.at[2]),
        pltpu.make_async_copy(momentum.at[1], state.at[2], in_sem.at[3]),
    ]
    for load in loads:
        load.start()
    matrix_s[...] = stencil_matrix()
    for load in loads:
        load.wait()

    def inverse_face(i):
        return 1.0 / jnp.full((8, LANES), face_s[i], jnp.float32)

    def reduce_step(i, carry):
        pairs, base = carry
        inv = inverse_face(i)
        inv_rows = jnp.concatenate([inv, inv], 0)
        base = [(u + g * inv, g) for u, g in base]
        phi[0, i] = base[0][0]
        phi[1, i] = base[1][0]
        base = [(u, g + u) for u, g in base]
        rho, m0, m1 = state[0, i], state[1, i], state[2, i]
        over = 1.0 / rho
        speed_y = m0 * over
        speed_z = m1 * over
        yy, yz, zz = m0 * speed_y, m1 * speed_y, m1 * speed_z
        flux_y[0, i, 8:24] = m0
        flux_y[1, i, 8:24] = yy
        flux_y[2, i, 8:24] = yz
        flux_zz[i] = zz
        out = []
        for (u, g), value in zip(pairs, (rho, m0, m1, yy, yz, zz)):
            u = u + g * inv_rows
            out.append((u, g + (u - value)))
        return out, base

    def reduce_steps(block, carry):
        for k in range(4):
            carry = reduce_step(4 * block + k, carry)
        return carry

    zero = jnp.zeros((16, LANES), jnp.float32)
    unit = jnp.ones((8, LANES), jnp.float32)
    pairs, base = lax.fori_loop(
        0,
        cells // 4,
        reduce_steps,
        ([(zero, zero)] * 6, [(unit, 0.0 * unit), (0.0 * unit, unit)]),
    )
    rho_r, m0_r, m1_r, yy_r, yz_r, zz_r = pairs
    plain = [value for pair in (rho_r, m0_r, m1_r) for value in pair]
    by_y = [value for pair in (m0_r, yy_r, yz_r) for value in pair]
    by_z = [value for pair in (m1_r, yz_r, zz_r) for value in pair]
    for k in range(6):
        reduced_y[k, 8:24] = by_y[k]
    z_pack[cells // 2] = pack_lanes(tiles_of(by_z))

    pl.semaphore_wait(barrier, len(near))

    def halo(which, source, target, axis, count, offset):
        return pltpu.make_async_remote_copy(
            source,
            target,
            halo_send.at[which],
            halo_recv.at[which],
            device_id=neighbour(axis, count, offset),
            device_id_type=MESH,
        )

    last = cells // 2
    near_halos = [
        halo(0, reduced_y.at[:, 21:24], reduced_y.at[:, 5:8], "gy", ny, 1),
        halo(1, reduced_y.at[:, 8:11], reduced_y.at[:, 24:27], "gy", ny, -1),
        halo(2, z_pack.at[last], z_left.at[last], "gz", nz, 1),
        halo(3, z_pack.at[last], z_right.at[last], "gz", nz, -1),
    ]
    for copy in near_halos:
        copy.start()
    for offset in (NEAR, -NEAR):
        pl.semaphore_signal(
            far_sem, inc=1, device_id=neighbour("gx", nx, offset), device_id_type=MESH
        )
    raw_y = [
        halo(4, flux_y.at[:, :, 21:24], flux_y.at[:, :, 5:8], "gy", ny, 1),
        halo(5, flux_y.at[:, :, 8:11], flux_y.at[:, :, 24:27], "gy", ny, -1),
    ]
    for copy in raw_y:
        copy.start()

    (u1, g1), (u2, g2) = base
    quarter = lax.broadcasted_iota(jnp.int32, (8, LANES), 1) // 32
    row6 = jnp.where(
        quarter < 2,
        jnp.where(quarter == 0, u1, u2),
        jnp.where(quarter == 2, g1, inverse_face(cells - 1)),
    )
    for h in range(2):
        send_a[pl.ds(64 * h + 6, 8, stride=8), :] = row6

    def pack_step(p, _):
        planes = []
        for q in range(2):
            i = 2 * p + q
            planes += [state[2, i], flux_y[2, i, 8:24], flux_zz[i]]
        z_pack[p] = pack_lanes(tiles_of(planes))
        return _

    lax.fori_loop(0, last, pack_step, 0)
    raw_z = [
        halo(6, z_pack.at[0:last], z_left.at[0:last], "gz", nz, 1),
        halo(7, z_pack.at[0:last], z_right.at[0:last], "gz", nz, -1),
    ]
    for copy in raw_z:
        copy.start()

    for copy in near_halos:
        copy.wait_recv()
    own_z = jnp.concatenate(by_z, 0)
    halo_z = jnp.concatenate(unpack_lanes(z_left[last], z_right[last], 12), 0)
    diff_z = along_z(own_z, halo_z, matrix_s[...])
    for f in range(3):
        for v in range(2):
            k = 2 * f + v
            diff_y = along_y(lambda step: reduced_y[k, pl.ds(8 + step, 16), :])
            value = plain[k] - SCALE * (diff_y + diff_z[16 * k : 16 * k + 16])
            for h in range(2):
                send_a[pl.ds(64 * h + 3 * v + f, 8, stride=8), :] = value[8 * h : 8 * h + 8]

    order = [k for step in range(nx // 2, 0, -1) for k in sorted({step, nx - step})]

    def rows(index, count):
        return pl.ds(pl.multiple_of(index * 8, 8), count)

    def exchange(source, target, count, send, recv, k):
        other = lax.rem(me + k, nx)
        return pltpu.make_async_remote_copy(
            source.at[rows(other, count)],
            target.at[rows(me, count)],
            send.at[k],
            recv.at[k],
            device_id={"gx": other},
            device_id_type=MESH,
        )

    pl.semaphore_wait(far_sem, 2)
    phase_a = [exchange(send_a, recv_a, 7, a_send, a_recv, k) for k in order]
    for copy in phase_a:
        copy.start()
    recv_a[rows(me, 7), :] = send_a[rows(me, 7), :]

    for copy in phase_a:
        copy.wait_recv()

    quarter = lax.broadcasted_iota(jnp.int32, (16, LANES), 1) // 32
    row6 = recv_a[pl.ds(6, 16, stride=8), :]
    turns = [row6] + [pltpu.roll(row6, 32 * k, 1) for k in (1, 2, 3)]

    def spread(which):
        odd = (quarter - which) & 1
        high = (quarter - which) & 2
        return jnp.where(
            high == 0,
            jnp.where(odd == 0, turns[0], turns[1]),
            jnp.where(odd == 0, turns[2], turns[3]),
        )

    t_uu, t_ug, t_gu = spread(0), spread(1), spread(2)
    coef[0] = t_uu
    coef[1] = t_ug
    coef[2] = t_gu
    coef[3] = (1.0 + t_ug * t_gu) / t_uu
    coef[4] = spread(3)

    def at_row(which, j):
        return jnp.broadcast_to(coef[which, pl.ds(j, 1), :], (3, LANES))

    blocks = [[at_row(which, j) for which in range(4)] for j in range(nx)]
    one = jnp.ones((3, LANES), jnp.float32)
    from_left = [(0.0 * one, one)]
    for j in range(nx):
        uu, ug, gu, gg = blocks[j]
        u, g = from_left[-1]
        from_left.append((uu * u + ug * g, gu * u + gg * g))
    from_right = [None] * nx + [(at_row(4, nx - 1), one)]
    for j in range(nx - 1, -1, -1):
        uu, ug, gu, gg = blocks[j]
        u, h = from_right[j + 1]
        from_right[j] = (gg * u + ug * h, gu * u + uu * h)
    norm = -1.0 / from_right[0][0]
    left_sums, right_terms = [0.0 * one], []
    for j in range(nx):
        u_r = recv_a[pl.ds(8 * j, 3), :]
        g_r = recv_a[pl.ds(8 * j + 3, 3), :]
        u, g = from_left[j + 1]
        left_sums.append(left_sums[-1] + (u * g_r - g * u_r))
        u, h = from_right[j + 1]
        right_terms.append(u * g_r + h * u_r)
    right_sum = 0.0 * one
    for d in range(nx - 1, -1, -1):
        right_sum = right_sum + right_terms[d]
        right, left = right_sum * norm, left_sums[d] * norm
        send_b[pl.ds(8 * d, 3), :] = right * from_left[d][0] + left * from_right[d][0]
        send_b[pl.ds(8 * d + 3, 3), :] = right * from_left[d][1] - left * from_right[d][1]

    phase_b = [exchange(send_b, recv_b, 6, b_send, b_recv, k) for k in order]
    for copy in phase_b:
        copy.start()
    recv_b[rows(me, 6), :] = send_b[rows(me, 6), :]

    for copy in raw_y + raw_z:
        copy.wait_recv()

    def local_step(p, carry):
        planes = []
        for q in range(2):
            i = 2 * p + q
            planes += [state[2, i], flux_y[2, i, 8:24], flux_zz[i]]
        halos = unpack_lanes(z_left[p], z_right[p], 12)
        diff_z = along_z(jnp.concatenate(planes, 0), jnp.concatenate(halos, 0), matrix_s[...])
        for q in range(2):
            i = 2 * p + q
            inv = inverse_face(i)
            inv_rows = jnp.concatenate([inv, inv], 0)
            new = []
            for f, (u, g) in enumerate(carry):
                diff_y = along_y(lambda step: flux_y[f, i, pl.ds(8 + step, 16), :])
                at = 16 * (3 * q + f)
                value = state[f, i] - SCALE * (diff_y + diff_z[at : at + 16])
                u = u + g * inv_rows
                local[f, i] = u
                new.append((u, g + (u - value)))
            carry = new
        return carry

    lax.fori_loop(0, last, local_step, [(zero, zero)] * 3)
    stores = [
        pltpu.make_async_copy(local, local_out, out_sem.at[0]),
        pltpu.make_async_copy(phi, phi_out, out_sem.at[1]),
    ]
    for store in stores:
        store.start()
    for copy in near_halos + raw_y + raw_z + phase_a:
        copy.wait_send()
    for store in stores:
        store.wait()
    for copy in phase_b:
        copy.wait_recv()
    for v in range(2):
        for f in range(3):
            ends_out[v, f] = recv_b[pl.ds(3 * v + f, 16, stride=8), :]
    for copy in phase_b:
        copy.wait_send()


def combine_kernel(local, phi, ends, out):
    starts = [(ends[0, f], ends[1, f]) for f in range(3)]
    for i in range(local.shape[1]):
        by_u = jnp.concatenate([phi[0, i]] * 2, 0)
        by_g = jnp.concatenate([phi[1, i]] * 2, 0)
        for f, (u, g) in enumerate(starts):
            out[f, i] = local[f, i] + (by_u * u + by_g * g)


def on_device(density, momentum, lower_face):
    counts = tuple(lax.axis_size(axis) for axis in ("gx", "gy", "gz"))
    nx = counts[0]
    cells, rows, lanes = density.shape
    block = (3, cells, rows, lanes)
    f32 = jnp.float32
    sems = pltpu.SemaphoreType.DMA
    local, phi, ends = pl.pallas_call(
        functools.partial(solve_kernel, counts),
        out_shape=(
            jax.ShapeDtypeStruct(block, f32),
            jax.ShapeDtypeStruct((2, cells, 8, lanes), f32),
            jax.ShapeDtypeStruct((2, 3, rows, lanes), f32),
        ),
        in_specs=[HBM, HBM, HBM],
        out_specs=(ANY, ANY, VMEM),
        scratch_shapes=[
            pltpu.SMEM((cells,), f32),
            pltpu.VMEM(block, f32),
            pltpu.VMEM((3, cells, 32, lanes), f32),
            pltpu.VMEM((cells, rows, lanes), f32),
            pltpu.VMEM((6, 32, lanes), f32),
            pltpu.VMEM((cells // 2 + 1, 8, lanes), f32),
            pltpu.VMEM((cells // 2 + 1, 8, lanes), f32),
            pltpu.VMEM((cells // 2 + 1, 8, lanes), f32),
            pltpu.VMEM((nx * 8, lanes), f32),
            pltpu.VMEM((nx * 8, lanes), f32),
            pltpu.VMEM((nx * 8, lanes), f32),
            pltpu.VMEM((nx * 8, lanes), f32),
            pltpu.VMEM((5, nx, lanes), f32),
            pltpu.VMEM((2 * lanes, lanes), jnp.bfloat16),
            pltpu.VMEM(block, f32),
            pltpu.VMEM((2, cells, 8, lanes), f32),
            sems((4,)),
            sems((8,)),
            sems((8,)),
            sems((nx,)),
            sems((nx,)),
            sems((nx,)),
            sems((nx,)),
            sems((2,)),
            pltpu.SemaphoreType.REGULAR,
        ],
        compiler_params=pltpu.CompilerParams(
            collective_id=0, has_side_effects=True, vmem_limit_bytes=16 << 20
        ),
        name="solve",
    )(*(pltpu.with_memory_space_constraint(x, pltpu.HBM) for x in (density, momentum, lower_face)))
    return pl.pallas_call(
        combine_kernel,
        out_shape=jax.ShapeDtypeStruct(block, f32),
        in_specs=[VMEM, VMEM, VMEM],
        out_specs=VMEM,
        compiler_params=pltpu.CompilerParams(vmem_limit_bytes=16 << 20),
        name="combine",
    )(local, phi, ends)


def solution(mesh):
    placed = (P("gx", "gy", "gz"), P(None, "gx", "gy", "gz"), P("gx"))
    return jax.shard_map(
        on_device, mesh=mesh, in_specs=placed, out_specs=P(None, "gx", "gy", "gz"), check_vma=False
    )
```

```python
import functools

import jax
import jax.numpy as jnp
from jax import lax
from jax.experimental import pallas as pl
from jax.experimental.pallas import tpu as pltpu
from jax.sharding import PartitionSpec as P

MESH = pl.DeviceIdType.MESH
ANY = pl.BlockSpec(memory_space=pl.ANY)
VMEM = pl.BlockSpec(memory_space=pltpu.VMEM)
HBM = pl.BlockSpec(memory_space=pltpu.HBM)
LANES = 128
WEIGHTS = (45.0, -9.0, 1.0)
SCALE = 0.2 / 60.0
NEAR = 4
OWNER_LIST = (11, 12, 14, 15, 0, 1, 3, 4)
OWNERS = 8
EACH = 2
SLOT = 16
A_ORDER = (0, 7, 1, 6, 2, 5, 3, 4)
B_ORDER = (0, 1, 2, 3, 4, 5, 6, 7, 15, 14, 13, 12, 8, 9, 10, 11)


def neighbour(axis, count, offset):
    return {axis: lax.rem(lax.axis_index(axis) + (offset + count), count)}


def stencil_matrix():
    source = lax.broadcasted_iota(jnp.int32, (2 * LANES, LANES), 0)
    target = lax.broadcasted_iota(jnp.int32, (2 * LANES, LANES), 1)
    own = source < LANES
    offset = jnp.where(own, source, source - LANES) - target
    matrix = jnp.zeros((2 * LANES, LANES), jnp.float32)
    for step, weight in enumerate(WEIGHTS, 1):
        for sign in (1, -1):
            inner = own & (offset == sign * step)
            wrapped = (source >= LANES) & (offset == sign * (step - LANES))
            matrix = jnp.where(inner | wrapped, sign * weight, matrix)
    return matrix.astype(jnp.bfloat16)


def along_z(own, halo, matrix):
    both = jnp.concatenate([own, halo], axis=1)
    high = both.astype(jnp.bfloat16)
    rest = both - high.astype(jnp.float32)
    middle = rest.astype(jnp.bfloat16)
    low = (rest - middle.astype(jnp.float32)).astype(jnp.bfloat16)
    dot = functools.partial(jnp.dot, preferred_element_type=jnp.float32)
    return dot(high, matrix) + (dot(middle, matrix) + dot(low, matrix))


def along_y(rows_at):
    total = None
    for step, weight in enumerate(WEIGHTS, 1):
        term = weight * (rows_at(step) - rows_at(-step))
        total = term if total is None else total + term
    return total


def pack_lanes(tiles):
    slot = lax.broadcasted_iota(jnp.int32, (8, LANES), 1) // 6
    packed = jnp.zeros((8, LANES), jnp.float32)
    for k, tile in enumerate(tiles):
        packed = jnp.where(slot == k, pltpu.roll(tile, 6 * k + 3, 1), packed)
    return packed


def unpack_lanes(from_left, from_right, count):
    lane = lax.broadcasted_iota(jnp.int32, (8, LANES), 1)
    both = jnp.where(lax.rem(lane, 6) < 3, from_left, from_right)
    return [pltpu.roll(both, (125 - 6 * k) % LANES, 1) for k in range(count)]


def tiles_of(planes):
    return [plane[8 * h : 8 * h + 8] for plane in planes for h in range(2)]


def own_rows(nx, mine, recv_a, send_b, recv_b, coef, to_owner, to_block, rows):
    me = lax.axis_index("gx")
    for j in range(nx):
        pl.when(me != j)(to_owner(0, j).wait_recv)
    quarter = lax.broadcasted_iota(jnp.int32, (nx, LANES), 1) // 32
    row6 = recv_a[pl.ds(6 * EACH, nx, stride=SLOT), :]
    turns = [row6] + [pltpu.roll(row6, 32 * k, 1) for k in (1, 2, 3)]

    def spread(which):
        odd = (quarter - which) & 1
        high = (quarter - which) & 2
        return jnp.where(
            high == 0,
            jnp.where(odd == 0, turns[0], turns[1]),
            jnp.where(odd == 0, turns[2], turns[3]),
        )

    t_uu, t_ug, t_gu = spread(0), spread(1), spread(2)
    coef[0] = t_uu
    coef[1] = t_ug
    coef[2] = t_gu
    coef[3] = (1.0 + t_ug * t_gu) / t_uu
    coef[4] = spread(3)

    def at_row(which, j):
        return jnp.broadcast_to(coef[which, pl.ds(j, 1), :], (3 * EACH, LANES))

    blocks = [[at_row(which, j) for which in range(4)] for j in range(nx)]
    one = jnp.ones((3 * EACH, LANES), jnp.float32)
    from_left = [(0.0 * one, one)]
    for j in range(nx):
        uu, ug, gu, gg = blocks[j]
        u, g = from_left[-1]
        from_left.append((uu * u + ug * g, gu * u + gg * g))
    from_right = [None] * nx + [(at_row(4, nx - 1), one)]
    for j in range(nx - 1, -1, -1):
        uu, ug, gu, gg = blocks[j]
        u, h = from_right[j + 1]
        from_right[j] = (gg * u + ug * h, gu * u + uu * h)
    norm = -1.0 / from_right[0][0]
    left_sums, right_terms = [0.0 * one], []
    for j in range(nx):
        u_r = recv_a[pl.ds(SLOT * j, 3 * EACH), :]
        g_r = recv_a[pl.ds(SLOT * j + 3 * EACH, 3 * EACH), :]
        u, g = from_left[j + 1]
        left_sums.append(left_sums[-1] + (u * g_r - g * u_r))
        u, h = from_right[j + 1]
        right_terms.append(u * g_r + h * u_r)
    right_sum = 0.0 * one
    for d in range(nx - 1, -1, -1):
        right_sum = right_sum + right_terms[d]
        right, left = right_sum * norm, left_sums[d] * norm
        send_b[pl.ds(SLOT * d, 3 * EACH), :] = right * from_left[d][0] + left * from_right[d][0]
        send_b[pl.ds(SLOT * d + 3 * EACH, 3 * EACH), :] = right * from_left[d][1] - left * from_right[d][1]
    for d in B_ORDER:
        pl.when(me != d)(to_block(mine, d).start)

        @pl.when(me == d)
        def _():
            recv_b[rows(mine, 6 * EACH), :] = send_b[rows(d, 6 * EACH), :]


def solve_kernel(
    counts,
    density,
    momentum,
    face,
    local_out,
    phi_out,
    ends_out,
    face_s,
    state,
    flux_y,
    flux_zz,
    reduced_y,
    z_pack,
    z_left,
    z_right,
    send_a,
    recv_a,
    send_b,
    recv_b,
    coef,
    matrix_s,
    local,
    phi,
    in_sem,
    halo_send,
    halo_recv,
    a_send,
    a_recv,
    b_send,
    b_recv,
    out_sem,
    far_sem,
):
    nx, ny, nz = counts
    cells = state.shape[1]
    me = lax.axis_index("gx")

    barrier = pltpu.get_barrier_semaphore()
    near = [("gx", nx, k) for step in range(NEAR, 0, -1) for k in (step, -step)]
    near += [("gy", ny, 1), ("gy", ny, -1), ("gz", nz, 1), ("gz", nz, -1)]
    for axis, count, offset in near:
        pl.semaphore_signal(
            barrier, inc=1, device_id=neighbour(axis, count, offset), device_id_type=MESH
        )
    loads = [
        pltpu.make_async_copy(face, face_s, in_sem.at[0]),
        pltpu.make_async_copy(density, state.at[0], in_sem.at[1]),
        pltpu.make_async_copy(momentum.at[0], state.at[1], in_sem.at[2]),
        pltpu.make_async_copy(momentum.at[1], state.at[2], in_sem.at[3]),
    ]
    for load in loads:
        load.start()
    matrix_s[...] = stencil_matrix()
    for load in loads:
        load.wait()

    def inverse_face(i):
        return 1.0 / jnp.full((8, LANES), face_s[i], jnp.float32)

    def reduce_step(i, carry):
        pairs, base = carry
        inv = inverse_face(i)
        inv_rows = jnp.concatenate([inv, inv], 0)
        base = [(u + g * inv, g) for u, g in base]
        phi[0, i] = base[0][0]
        phi[1, i] = base[1][0]
        base = [(u, g + u) for u, g in base]
        rho, m0, m1 = state[0, i], state[1, i], state[2, i]
        over = 1.0 / rho
        speed_y = m0 * over
        speed_z = m1 * over
        yy, yz, zz = m0 * speed_y, m1 * speed_y, m1 * speed_z
        flux_y[0, i, 8:24] = m0
        flux_y[1, i, 8:24] = yy
        flux_y[2, i, 8:24] = yz
        flux_zz[i] = zz
        out = []
        for (u, g), value in zip(pairs, (rho, m0, m1, yy, yz, zz)):
            u = u + g * inv_rows
            out.append((u, g + (u - value)))
        return out, base

    def reduce_steps(block, carry):
        for k in range(4):
            carry = reduce_step(4 * block + k, carry)
        return carry

    zero = jnp.zeros((16, LANES), jnp.float32)
    unit = jnp.ones((8, LANES), jnp.float32)
    pairs, base = lax.fori_loop(
        0,
        cells // 4,
        reduce_steps,
        ([(zero, zero)] * 6, [(unit, 0.0 * unit), (0.0 * unit, unit)]),
    )
    rho_r, m0_r, m1_r, yy_r, yz_r, zz_r = pairs
    plain = [value for pair in (rho_r, m0_r, m1_r) for value in pair]
    by_y = [value for pair in (m0_r, yy_r, yz_r) for value in pair]
    by_z = [value for pair in (m1_r, yz_r, zz_r) for value in pair]
    for k in range(6):
        reduced_y[k, 8:24] = by_y[k]
    z_pack[cells // 2] = pack_lanes(tiles_of(by_z))

    pl.semaphore_wait(barrier, len(near))
    for offset in (NEAR, -NEAR):
        pl.semaphore_signal(
            far_sem, inc=1, device_id=neighbour("gx", nx, offset), device_id_type=MESH
        )

    def halo(which, source, target, axis, count, offset):
        return pltpu.make_async_remote_copy(
            source,
            target,
            halo_send.at[which],
            halo_recv.at[which],
            device_id=neighbour(axis, count, offset),
            device_id_type=MESH,
        )

    last = cells // 2
    near_halos = [
        halo(0, reduced_y.at[:, 21:24], reduced_y.at[:, 5:8], "gy", ny, 1),
        halo(1, reduced_y.at[:, 8:11], reduced_y.at[:, 24:27], "gy", ny, -1),
        halo(2, z_pack.at[last], z_left.at[last], "gz", nz, 1),
        halo(3, z_pack.at[last], z_right.at[last], "gz", nz, -1),
    ]
    for copy in near_halos:
        copy.start()
    raw_y = [
        halo(4, flux_y.at[:, :, 21:24], flux_y.at[:, :, 5:8], "gy", ny, 1),
        halo(5, flux_y.at[:, :, 8:11], flux_y.at[:, :, 24:27], "gy", ny, -1),
    ]
    for copy in raw_y:
        copy.start()

    (u1, g1), (u2, g2) = base
    quarter = lax.broadcasted_iota(jnp.int32, (8, LANES), 1) // 32
    row6 = jnp.where(
        quarter < 2,
        jnp.where(quarter == 0, u1, u2),
        jnp.where(quarter == 2, g1, inverse_face(cells - 1)),
    )
    send_a[pl.ds(6 * EACH, OWNERS, stride=SLOT), :] = jnp.concatenate([row6] * (OWNERS // 8), 0)

    def pack_step(p, _):
        planes = []
        for q in range(2):
            i = 2 * p + q
            planes += [state[2, i], flux_y[2, i, 8:24], flux_zz[i]]
        z_pack[p] = pack_lanes(tiles_of(planes))
        return _

    lax.fori_loop(0, last, pack_step, 0)
    raw_z = [
        halo(6, z_pack.at[0:last], z_left.at[0:last], "gz", nz, 1),
        halo(7, z_pack.at[0:last], z_right.at[0:last], "gz", nz, -1),
    ]
    for copy in raw_z:
        copy.start()

    for copy in near_halos:
        copy.wait_recv()
    own_z = jnp.concatenate(by_z, 0)
    halo_z = jnp.concatenate(unpack_lanes(z_left[last], z_right[last], 12), 0)
    diff_z = along_z(own_z, halo_z, matrix_s[...])
    for f in range(3):
        for v in range(2):
            k = 2 * f + v
            diff_y = along_y(lambda step: reduced_y[k, pl.ds(8 + step, 16), :])
            value = plain[k] - SCALE * (diff_y + diff_z[16 * k : 16 * k + 16])
            for r in range(EACH):
                at = EACH * (3 * v + f) + r
                part = value[OWNERS * r : OWNERS * (r + 1)]
                send_a[pl.ds(at, OWNERS, stride=SLOT), :] = part

    def rows(index, count):
        return pl.ds(pl.multiple_of(index * SLOT, 8), count)

    owners = OWNER_LIST
    mine = sum(c * (me == owner).astype(jnp.int32) for c, owner in enumerate(owners))
    is_owner = functools.reduce(jnp.logical_or, [me == owner for owner in owners])

    def to_owner(c, source):
        return pltpu.make_async_remote_copy(
            send_a.at[rows(c, 6 * EACH + 1)],
            recv_a.at[rows(source, 6 * EACH + 1)],
            a_send.at[c],
            a_recv.at[source],
            device_id={"gx": owners[c]},
            device_id_type=MESH,
        )

    def to_block(c, target):
        return pltpu.make_async_remote_copy(
            send_b.at[rows(target, 6 * EACH)],
            recv_b.at[rows(c, 6 * EACH)],
            b_send.at[target],
            b_recv.at[c],
            device_id={"gx": target},
            device_id_type=MESH,
        )

    pl.semaphore_wait(far_sem, 2)
    for c in A_ORDER:
        pl.when(me != owners[c])(to_owner(c, me).start)

        @pl.when(me == owners[c])
        def _():
            recv_a[rows(me, 6 * EACH + 1), :] = send_a[rows(c, 6 * EACH + 1), :]

    for copy in raw_y + raw_z:
        copy.wait_recv()

    def local_step(p, carry):
        planes = []
        for q in range(2):
            i = 2 * p + q
            planes += [state[2, i], flux_y[2, i, 8:24], flux_zz[i]]
        halos = unpack_lanes(z_left[p], z_right[p], 12)
        diff_z = along_z(jnp.concatenate(planes, 0), jnp.concatenate(halos, 0), matrix_s[...])
        for q in range(2):
            i = 2 * p + q
            inv = inverse_face(i)
            inv_rows = jnp.concatenate([inv, inv], 0)
            new = []
            for f, (u, g) in enumerate(carry):
                diff_y = along_y(lambda step: flux_y[f, i, pl.ds(8 + step, 16), :])
                at = 16 * (3 * q + f)
                value = state[f, i] - SCALE * (diff_y + diff_z[at : at + 16])
                u = u + g * inv_rows
                local[f, i] = u
                new.append((u, g + (u - value)))
            carry = new
        return carry

    lax.fori_loop(0, last, local_step, [(zero, zero)] * 3)
    stores = [
        pltpu.make_async_copy(local, local_out, out_sem.at[0]),
        pltpu.make_async_copy(phi, phi_out, out_sem.at[1]),
    ]
    for store in stores:
        store.start()

    @pl.when(is_owner)
    def _():
        own_rows(nx, mine, recv_a, send_b, recv_b, coef, to_owner, to_block, rows)

    for copy in near_halos + raw_y + raw_z:
        copy.wait_send()
    for store in stores:
        store.wait()
    for c in range(OWNERS):
        pl.when(me != owners[c])(to_block(c, me).wait_recv)
    for v in range(2):
        for f in range(3):
            for r in range(EACH):
                at = EACH * (3 * v + f) + r
                part = recv_b[pl.ds(at, OWNERS, stride=SLOT), :]
                ends_out[v, f, OWNERS * r : OWNERS * (r + 1)] = part
    for c in range(OWNERS):
        pl.when(me != owners[c])(to_owner(c, me).wait_send)
    for d in range(nx):
        pl.when(is_owner & (me != d))(to_block(mine, d).wait_send)


def combine_kernel(local, phi, ends, out):
    starts = [(ends[0, f], ends[1, f]) for f in range(3)]
    for i in range(local.shape[1]):
        by_u = jnp.concatenate([phi[0, i]] * 2, 0)
        by_g = jnp.concatenate([phi[1, i]] * 2, 0)
        for f, (u, g) in enumerate(starts):
            out[f, i] = local[f, i] + (by_u * u + by_g * g)


def on_device(density, momentum, lower_face):
    counts = tuple(lax.axis_size(axis) for axis in ("gx", "gy", "gz"))
    nx = counts[0]
    cells, rows, lanes = density.shape
    block = (3, cells, rows, lanes)
    f32 = jnp.float32
    sems = pltpu.SemaphoreType.DMA
    local, phi, ends = pl.pallas_call(
        functools.partial(solve_kernel, counts),
        out_shape=(
            jax.ShapeDtypeStruct(block, f32),
            jax.ShapeDtypeStruct((2, cells, 8, lanes), f32),
            jax.ShapeDtypeStruct((2, 3, rows, lanes), f32),
        ),
        in_specs=[HBM, HBM, HBM],
        out_specs=(ANY, ANY, VMEM),
        scratch_shapes=[
            pltpu.SMEM((cells,), f32),
            pltpu.VMEM(block, f32),
            pltpu.VMEM((3, cells, 32, lanes), f32),
            pltpu.VMEM((cells, rows, lanes), f32),
            pltpu.VMEM((6, 32, lanes), f32),
            pltpu.VMEM((cells // 2 + 1, 8, lanes), f32),
            pltpu.VMEM((cells // 2 + 1, 8, lanes), f32),
            pltpu.VMEM((cells // 2 + 1, 8, lanes), f32),
            pltpu.VMEM((OWNERS * SLOT, lanes), f32),
            pltpu.VMEM((nx * SLOT, lanes), f32),
            pltpu.VMEM((nx * SLOT, lanes), f32),
            pltpu.VMEM((OWNERS * SLOT, lanes), f32),
            pltpu.VMEM((5, nx, lanes), f32),
            pltpu.VMEM((2 * lanes, lanes), jnp.bfloat16),
            pltpu.VMEM(block, f32),
            pltpu.VMEM((2, cells, 8, lanes), f32),
            sems((4,)),
            sems((8,)),
            sems((8,)),
            sems((nx,)),
            sems((nx,)),
            sems((nx,)),
            sems((nx,)),
            sems((2,)),
            pltpu.SemaphoreType.REGULAR,
        ],
        compiler_params=pltpu.CompilerParams(
            collective_id=0, has_side_effects=True, vmem_limit_bytes=16 << 20
        ),
        name="solve",
    )(*(pltpu.with_memory_space_constraint(x, pltpu.HBM) for x in (density, momentum, lower_face)))
    return pl.pallas_call(
        combine_kernel,
        out_shape=jax.ShapeDtypeStruct(block, f32),
        in_specs=[VMEM, VMEM, VMEM],
        out_specs=VMEM,
        compiler_params=pltpu.CompilerParams(vmem_limit_bytes=16 << 20),
        name="combine",
    )(local, phi, ends)


def solution(mesh):
    placed = (P("gx", "gy", "gz"), P(None, "gx", "gy", "gz"), P("gx"))
    return jax.shard_map(
        on_device, mesh=mesh, in_specs=placed, out_specs=P(None, "gx", "gy", "gz"), check_vma=False
    )
```

```python
import functools

import jax
import jax.numpy as jnp
from jax import lax
from jax.experimental import pallas as pl
from jax.experimental.pallas import tpu as pltpu
from jax.sharding import PartitionSpec as P

MESH = pl.DeviceIdType.MESH
ANY = pl.BlockSpec(memory_space=pl.ANY)
VMEM = pl.BlockSpec(memory_space=pltpu.VMEM)
HBM = pl.BlockSpec(memory_space=pltpu.HBM)
LANES = 128
WEIGHTS = (45.0, -9.0, 1.0)
SCALE = 0.2 / 60.0
NEAR = 4
PARTS = 4
OWNER_LIST = (11, 12, 14, 15, 0, 1, 3, 4)
OWNERS = 8
EACH = 2
SLOT = 16
A_ORDER = (0, 7, 1, 6, 2, 5, 3, 4)
B_ORDER = (0, 1, 2, 3, 4, 5, 6, 7, 15, 14, 13, 12, 8, 9, 10, 11)


def neighbour(axis, count, offset):
    return {axis: lax.rem(lax.axis_index(axis) + (offset + count), count)}


def stencil_matrix():
    source = lax.broadcasted_iota(jnp.int32, (2 * LANES, LANES), 0)
    target = lax.broadcasted_iota(jnp.int32, (2 * LANES, LANES), 1)
    own = source < LANES
    offset = jnp.where(own, source, source - LANES) - target
    matrix = jnp.zeros((2 * LANES, LANES), jnp.float32)
    for step, weight in enumerate(WEIGHTS, 1):
        for sign in (1, -1):
            inner = own & (offset == sign * step)
            wrapped = (source >= LANES) & (offset == sign * (step - LANES))
            matrix = jnp.where(inner | wrapped, sign * weight, matrix)
    return matrix.astype(jnp.bfloat16)


def along_z(own, halo, matrix):
    both = jnp.concatenate([own, halo], axis=1)
    high = both.astype(jnp.bfloat16)
    rest = both - high.astype(jnp.float32)
    middle = rest.astype(jnp.bfloat16)
    low = (rest - middle.astype(jnp.float32)).astype(jnp.bfloat16)
    dot = functools.partial(jnp.dot, preferred_element_type=jnp.float32)
    return dot(high, matrix) + (dot(middle, matrix) + dot(low, matrix))


def along_y(rows_at):
    total = None
    for step, weight in enumerate(WEIGHTS, 1):
        term = weight * (rows_at(step) - rows_at(-step))
        total = term if total is None else total + term
    return total


def pack_lanes(tiles):
    slot = lax.broadcasted_iota(jnp.int32, (8, LANES), 1) // 6
    packed = jnp.zeros((8, LANES), jnp.float32)
    for k, tile in enumerate(tiles):
        packed = jnp.where(slot == k, pltpu.roll(tile, 6 * k + 3, 1), packed)
    return packed


def unpack_lanes(from_left, from_right, count):
    lane = lax.broadcasted_iota(jnp.int32, (8, LANES), 1)
    both = jnp.where(lax.rem(lane, 6) < 3, from_left, from_right)
    return [pltpu.roll(both, (125 - 6 * k) % LANES, 1) for k in range(count)]


def tiles_of(planes):
    return [plane[8 * h : 8 * h + 8] for plane in planes for h in range(2)]


def own_rows(nx, mine, recv_a, send_b, recv_b, coef, to_owner, to_block, rows):
    me = lax.axis_index("gx")
    for j in range(nx):
        pl.when(me != j)(to_owner(0, j).wait_recv)
    quarter = lax.broadcasted_iota(jnp.int32, (nx, LANES), 1) // 32
    row6 = recv_a[pl.ds(6 * EACH, nx, stride=SLOT), :]
    turns = [row6] + [pltpu.roll(row6, 32 * k, 1) for k in (1, 2, 3)]

    def spread(which):
        odd = (quarter - which) & 1
        high = (quarter - which) & 2
        return jnp.where(
            high == 0,
            jnp.where(odd == 0, turns[0], turns[1]),
            jnp.where(odd == 0, turns[2], turns[3]),
        )

    t_uu, t_ug, t_gu = spread(0), spread(1), spread(2)
    coef[0] = t_uu
    coef[1] = t_ug
    coef[2] = t_gu
    coef[3] = (1.0 + t_ug * t_gu) / t_uu
    coef[4] = spread(3)

    def at_row(which, j):
        return jnp.broadcast_to(coef[which, pl.ds(j, 1), :], (3 * EACH, LANES))

    blocks = [[at_row(which, j) for which in range(4)] for j in range(nx)]
    one = jnp.ones((3 * EACH, LANES), jnp.float32)
    from_left = [(0.0 * one, one)]
    for j in range(nx):
        uu, ug, gu, gg = blocks[j]
        u, g = from_left[-1]
        from_left.append((uu * u + ug * g, gu * u + gg * g))
    from_right = [None] * nx + [(at_row(4, nx - 1), one)]
    for j in range(nx - 1, -1, -1):
        uu, ug, gu, gg = blocks[j]
        u, h = from_right[j + 1]
        from_right[j] = (gg * u + ug * h, gu * u + uu * h)
    norm = -1.0 / from_right[0][0]
    left_sums, right_terms = [0.0 * one], []
    for j in range(nx):
        u_r = recv_a[pl.ds(SLOT * j, 3 * EACH), :]
        g_r = recv_a[pl.ds(SLOT * j + 3 * EACH, 3 * EACH), :]
        u, g = from_left[j + 1]
        left_sums.append(left_sums[-1] + (u * g_r - g * u_r))
        u, h = from_right[j + 1]
        right_terms.append(u * g_r + h * u_r)
    right_sum = 0.0 * one
    for d in range(nx - 1, -1, -1):
        right_sum = right_sum + right_terms[d]
        right, left = right_sum * norm, left_sums[d] * norm
        send_b[pl.ds(SLOT * d, 3 * EACH), :] = right * from_left[d][0] + left * from_right[d][0]
        send_b[pl.ds(SLOT * d + 3 * EACH, 3 * EACH), :] = right * from_left[d][1] - left * from_right[d][1]
    for d in B_ORDER:
        pl.when(me != d)(to_block(mine, d).start)

        @pl.when(me == d)
        def _():
            recv_b[rows(mine, 6 * EACH), :] = send_b[rows(d, 6 * EACH), :]


def solve_kernel(
    counts,
    density,
    momentum,
    face,
    local_out,
    phi_out,
    ends_out,
    face_s,
    state,
    flux_y,
    flux_zz,
    reduced_y,
    z_pack,
    z_left,
    z_right,
    send_a,
    recv_a,
    send_b,
    recv_b,
    coef,
    matrix_s,
    local,
    phi,
    in_sem,
    halo_send,
    halo_recv,
    a_send,
    a_recv,
    b_send,
    b_recv,
    out_sem,
    far_sem,
):
    nx, ny, nz = counts
    cells = state.shape[1]
    me = lax.axis_index("gx")

    barrier = pltpu.get_barrier_semaphore()
    near = [("gx", nx, k) for step in range(NEAR, 0, -1) for k in (step, -step)]
    near += [("gy", ny, 1), ("gy", ny, -1), ("gz", nz, 1), ("gz", nz, -1)]
    for axis, count, offset in near:
        pl.semaphore_signal(
            barrier, inc=1, device_id=neighbour(axis, count, offset), device_id_type=MESH
        )
    loads = [
        pltpu.make_async_copy(face, face_s, in_sem.at[0]),
        pltpu.make_async_copy(density, state.at[0], in_sem.at[1]),
        pltpu.make_async_copy(momentum.at[0], state.at[1], in_sem.at[2]),
        pltpu.make_async_copy(momentum.at[1], state.at[2], in_sem.at[3]),
    ]
    for load in loads:
        load.start()
    matrix_s[...] = stencil_matrix()
    for load in loads:
        load.wait()

    def inverse_face(i):
        return 1.0 / jnp.full((8, LANES), face_s[i], jnp.float32)

    def reduce_step(i, carry):
        pairs, base = carry
        inv = inverse_face(i)
        inv_rows = jnp.concatenate([inv, inv], 0)
        base = [(u + g * inv, g) for u, g in base]
        phi[0, i] = base[0][0]
        phi[1, i] = base[1][0]
        base = [(u, g + u) for u, g in base]
        rho, m0, m1 = state[0, i], state[1, i], state[2, i]
        over = 1.0 / rho
        speed_y = m0 * over
        speed_z = m1 * over
        yy, yz, zz = m0 * speed_y, m1 * speed_y, m1 * speed_z
        flux_y[0, i, 8:24] = m0
        flux_y[1, i, 8:24] = yy
        flux_y[2, i, 8:24] = yz
        flux_zz[i] = zz
        out = []
        for (u, g), value in zip(pairs, (rho, m0, m1, yy, yz, zz)):
            u = u + g * inv_rows
            out.append((u, g + (u - value)))
        return out, base

    def reduce_steps(block, carry):
        for k in range(4):
            carry = reduce_step(4 * block + k, carry)
        return carry

    zero = jnp.zeros((16, LANES), jnp.float32)
    unit = jnp.ones((8, LANES), jnp.float32)
    pairs, base = lax.fori_loop(
        0,
        cells // 4,
        reduce_steps,
        ([(zero, zero)] * 6, [(unit, 0.0 * unit), (0.0 * unit, unit)]),
    )
    rho_r, m0_r, m1_r, yy_r, yz_r, zz_r = pairs
    plain = [value for pair in (rho_r, m0_r, m1_r) for value in pair]
    by_y = [value for pair in (m0_r, yy_r, yz_r) for value in pair]
    by_z = [value for pair in (m1_r, yz_r, zz_r) for value in pair]
    for k in range(6):
        reduced_y[k, 8:24] = by_y[k]
    z_pack[cells // 2] = pack_lanes(tiles_of(by_z))

    pl.semaphore_wait(barrier, len(near))
    for offset in (NEAR, -NEAR):
        pl.semaphore_signal(
            far_sem, inc=1, device_id=neighbour("gx", nx, offset), device_id_type=MESH
        )

    def halo(which, source, target, axis, count, offset):
        return pltpu.make_async_remote_copy(
            source,
            target,
            halo_send.at[which],
            halo_recv.at[which],
            device_id=neighbour(axis, count, offset),
            device_id_type=MESH,
        )

    last = cells // 2
    near_halos = [
        halo(0, reduced_y.at[:, 21:24], reduced_y.at[:, 5:8], "gy", ny, 1),
        halo(1, reduced_y.at[:, 8:11], reduced_y.at[:, 24:27], "gy", ny, -1),
        halo(2, z_pack.at[last], z_left.at[last], "gz", nz, 1),
        halo(3, z_pack.at[last], z_right.at[last], "gz", nz, -1),
    ]
    for copy in near_halos:
        copy.start()
    raw_y = [
        halo(4, flux_y.at[:, :, 21:24], flux_y.at[:, :, 5:8], "gy", ny, 1),
        halo(5, flux_y.at[:, :, 8:11], flux_y.at[:, :, 24:27], "gy", ny, -1),
    ]
    for copy in raw_y:
        copy.start()

    (u1, g1), (u2, g2) = base
    quarter = lax.broadcasted_iota(jnp.int32, (8, LANES), 1) // 32
    row6 = jnp.where(
        quarter < 2,
        jnp.where(quarter == 0, u1, u2),
        jnp.where(quarter == 2, g1, inverse_face(cells - 1)),
    )
    send_a[pl.ds(6 * EACH, OWNERS, stride=SLOT), :] = jnp.concatenate([row6] * (OWNERS // 8), 0)

    def pack_step(p, _):
        planes = []
        for q in range(2):
            i = 2 * p + q
            planes += [state[2, i], flux_y[2, i, 8:24], flux_zz[i]]
        z_pack[p] = pack_lanes(tiles_of(planes))
        return _

    lax.fori_loop(0, last, pack_step, 0)
    raw_z = [
        halo(6, z_pack.at[0:last], z_left.at[0:last], "gz", nz, 1),
        halo(7, z_pack.at[0:last], z_right.at[0:last], "gz", nz, -1),
    ]
    for copy in raw_z:
        copy.start()

    for copy in near_halos:
        copy.wait_recv()
    own_z = jnp.concatenate(by_z, 0)
    halo_z = jnp.concatenate(unpack_lanes(z_left[last], z_right[last], 12), 0)
    diff_z = along_z(own_z, halo_z, matrix_s[...])
    for f in range(3):
        for v in range(2):
            k = 2 * f + v
            diff_y = along_y(lambda step: reduced_y[k, pl.ds(8 + step, 16), :])
            value = plain[k] - SCALE * (diff_y + diff_z[16 * k : 16 * k + 16])
            for r in range(EACH):
                at = EACH * (3 * v + f) + r
                part = value[OWNERS * r : OWNERS * (r + 1)]
                send_a[pl.ds(at, OWNERS, stride=SLOT), :] = part

    def rows(index, count):
        return pl.ds(pl.multiple_of(index * SLOT, 8), count)

    owners = OWNER_LIST
    mine = sum(c * (me == owner).astype(jnp.int32) for c, owner in enumerate(owners))
    is_owner = functools.reduce(jnp.logical_or, [me == owner for owner in owners])

    def to_owner(c, source):
        return pltpu.make_async_remote_copy(
            send_a.at[rows(c, 6 * EACH + 1)],
            recv_a.at[rows(source, 6 * EACH + 1)],
            a_send.at[c],
            a_recv.at[source],
            device_id={"gx": owners[c]},
            device_id_type=MESH,
        )

    def to_block(c, target):
        return pltpu.make_async_remote_copy(
            send_b.at[rows(target, 6 * EACH)],
            recv_b.at[rows(c, 6 * EACH)],
            b_send.at[target],
            b_recv.at[c],
            device_id={"gx": target},
            device_id_type=MESH,
        )

    pl.semaphore_wait(far_sem, 2)
    for c in A_ORDER:
        pl.when(me != owners[c])(to_owner(c, me).start)

        @pl.when(me == owners[c])
        def _():
            recv_a[rows(me, 6 * EACH + 1), :] = send_a[rows(c, 6 * EACH + 1), :]

    for copy in raw_y + raw_z:
        copy.wait_recv()

    def local_step(p, carry):
        planes = []
        for q in range(2):
            i = 2 * p + q
            planes += [state[2, i], flux_y[2, i, 8:24], flux_zz[i]]
        halos = unpack_lanes(z_left[p], z_right[p], 12)
        diff_z = along_z(jnp.concatenate(planes, 0), jnp.concatenate(halos, 0), matrix_s[...])
        for q in range(2):
            i = 2 * p + q
            inv = inverse_face(i)
            inv_rows = jnp.concatenate([inv, inv], 0)
            new = []
            for f, (u, g) in enumerate(carry):
                diff_y = along_y(lambda step: flux_y[f, i, pl.ds(8 + step, 16), :])
                at = 16 * (3 * q + f)
                value = state[f, i] - SCALE * (diff_y + diff_z[at : at + 16])
                u = u + g * inv_rows
                local[f, i] = u
                new.append((u, g + (u - value)))
            carry = new
        return carry

    lax.fori_loop(0, last, local_step, [(zero, zero)] * 3)
    stores = [
        pltpu.make_async_copy(local, local_out, out_sem.at[0]),
        pltpu.make_async_copy(phi, phi_out, out_sem.at[1]),
    ]
    for store in stores:
        store.start()

    @pl.when(is_owner)
    def _():
        own_rows(nx, mine, recv_a, send_b, recv_b, coef, to_owner, to_block, rows)

    for copy in near_halos + raw_y + raw_z:
        copy.wait_send()
    for store in stores:
        store.wait()
    for c in range(OWNERS):
        pl.when(me != owners[c])(to_block(c, me).wait_recv)
    for v in range(2):
        for f in range(3):
            for r in range(EACH):
                at = EACH * (3 * v + f) + r
                part = recv_b[pl.ds(at, OWNERS, stride=SLOT), :]
                ends_out[v, f, OWNERS * r : OWNERS * (r + 1)] = part
    for c in range(OWNERS):
        pl.when(me != owners[c])(to_owner(c, me).wait_send)
    for d in range(nx):
        pl.when(is_owner & (me != d))(to_block(mine, d).wait_send)


def combine_kernel(local, phi, ends, out, staged, sems):
    starts = [(ends[0, f], ends[1, f]) for f in range(3)]
    cells = local.shape[1]
    size = cells // PARTS
    stores = []
    for part in range(PARTS):
        span = pl.ds(part * size, size)
        for i in range(part * size, (part + 1) * size):
            by_u = jnp.concatenate([phi[0, i]] * 2, 0)
            by_g = jnp.concatenate([phi[1, i]] * 2, 0)
            for f, (u, g) in enumerate(starts):
                staged[f, i] = local[f, i] + (by_u * u + by_g * g)
        store = pltpu.make_async_copy(staged.at[:, span], out.at[:, span], sems.at[part])
        store.start()
        stores.append(store)
    for store in stores:
        store.wait()


def on_device(density, momentum, lower_face):
    counts = tuple(lax.axis_size(axis) for axis in ("gx", "gy", "gz"))
    nx = counts[0]
    cells, rows, lanes = density.shape
    block = (3, cells, rows, lanes)
    f32 = jnp.float32
    sems = pltpu.SemaphoreType.DMA
    local, phi, ends = pl.pallas_call(
        functools.partial(solve_kernel, counts),
        out_shape=(
            jax.ShapeDtypeStruct(block, f32),
            jax.ShapeDtypeStruct((2, cells, 8, lanes), f32),
            jax.ShapeDtypeStruct((2, 3, rows, lanes), f32),
        ),
        in_specs=[HBM, HBM, HBM],
        out_specs=(ANY, ANY, VMEM),
        scratch_shapes=[
            pltpu.SMEM((cells,), f32),
            pltpu.VMEM(block, f32),
            pltpu.VMEM((3, cells, 32, lanes), f32),
            pltpu.VMEM((cells, rows, lanes), f32),
            pltpu.VMEM((6, 32, lanes), f32),
            pltpu.VMEM((cells // 2 + 1, 8, lanes), f32),
            pltpu.VMEM((cells // 2 + 1, 8, lanes), f32),
            pltpu.VMEM((cells // 2 + 1, 8, lanes), f32),
            pltpu.VMEM((OWNERS * SLOT, lanes), f32),
            pltpu.VMEM((nx * SLOT, lanes), f32),
            pltpu.VMEM((nx * SLOT, lanes), f32),
            pltpu.VMEM((OWNERS * SLOT, lanes), f32),
            pltpu.VMEM((5, nx, lanes), f32),
            pltpu.VMEM((2 * lanes, lanes), jnp.bfloat16),
            pltpu.VMEM(block, f32),
            pltpu.VMEM((2, cells, 8, lanes), f32),
            sems((4,)),
            sems((8,)),
            sems((8,)),
            sems((nx,)),
            sems((nx,)),
            sems((nx,)),
            sems((nx,)),
            sems((2,)),
            pltpu.SemaphoreType.REGULAR,
        ],
        compiler_params=pltpu.CompilerParams(
            collective_id=0, has_side_effects=True, vmem_limit_bytes=16 << 20
        ),
        name="solve",
    )(*(pltpu.with_memory_space_constraint(x, pltpu.HBM) for x in (density, momentum, lower_face)))
    return pl.pallas_call(
        combine_kernel,
        out_shape=jax.ShapeDtypeStruct(block, f32),
        in_specs=[VMEM, VMEM, VMEM],
        out_specs=ANY,
        scratch_shapes=[pltpu.VMEM(block, f32), sems((PARTS,))],
        compiler_params=pltpu.CompilerParams(vmem_limit_bytes=16 << 20),
        name="combine",
    )(local, phi, ends)


def solution(mesh):
    placed = (P("gx", "gy", "gz"), P(None, "gx", "gy", "gz"), P("gx"))
    return jax.shard_map(
        on_device, mesh=mesh, in_specs=placed, out_specs=P(None, "gx", "gy", "gz"), check_vma=False
    )
```

```python
import functools

import jax
import jax.numpy as jnp
from jax import lax
from jax.experimental import pallas as pl
from jax.experimental.pallas import tpu as pltpu
from jax.sharding import PartitionSpec as P

MESH = pl.DeviceIdType.MESH
ANY = pl.BlockSpec(memory_space=pl.ANY)
VMEM = pl.BlockSpec(memory_space=pltpu.VMEM)
HBM = pl.BlockSpec(memory_space=pltpu.HBM)
LANES = 128
WEIGHTS = (45.0, -9.0, 1.0)
SCALE = 0.2 / 60.0
NEAR = 4
PARTS = 4
OWNER_LIST = (11, 12, 14, 15, 0, 1, 3, 4)
OWNERS = 8
EACH = 2
SLOT = 16
LATE_OWNERS = (0, 1, 2, 3)
EARLY_OWNERS = (7, 6, 5, 4)
B_ORDER = (0, 1, 2, 3, 4, 5, 6, 7, 15, 14, 13, 12, 8, 9, 10, 11)


def neighbour(axis, count, offset):
    return {axis: lax.rem(lax.axis_index(axis) + (offset + count), count)}


def stencil_matrix():
    source = lax.broadcasted_iota(jnp.int32, (2 * LANES, LANES), 0)
    target = lax.broadcasted_iota(jnp.int32, (2 * LANES, LANES), 1)
    own = source < LANES
    offset = jnp.where(own, source, source - LANES) - target
    matrix = jnp.zeros((2 * LANES, LANES), jnp.float32)
    for step, weight in enumerate(WEIGHTS, 1):
        for sign in (1, -1):
            inner = own & (offset == sign * step)
            wrapped = (source >= LANES) & (offset == sign * (step - LANES))
            matrix = jnp.where(inner | wrapped, sign * weight, matrix)
    return matrix.astype(jnp.bfloat16)


def along_z(own, halo, matrix):
    both = jnp.concatenate([own, halo], axis=1)
    high = both.astype(jnp.bfloat16)
    rest = both - high.astype(jnp.float32)
    middle = rest.astype(jnp.bfloat16)
    low = (rest - middle.astype(jnp.float32)).astype(jnp.bfloat16)
    dot = functools.partial(jnp.dot, preferred_element_type=jnp.float32)
    return dot(high, matrix) + (dot(middle, matrix) + dot(low, matrix))


def along_y(rows_at):
    total = None
    for step, weight in enumerate(WEIGHTS, 1):
        term = weight * (rows_at(step) - rows_at(-step))
        total = term if total is None else total + term
    return total


def pack_lanes(tiles):
    slot = lax.broadcasted_iota(jnp.int32, (8, LANES), 1) // 6
    packed = jnp.zeros((8, LANES), jnp.float32)
    for k, tile in enumerate(tiles):
        packed = jnp.where(slot == k, pltpu.roll(tile, 6 * k + 3, 1), packed)
    return packed


def unpack_lanes(from_left, from_right, count):
    lane = lax.broadcasted_iota(jnp.int32, (8, LANES), 1)
    both = jnp.where(lax.rem(lane, 6) < 3, from_left, from_right)
    return [pltpu.roll(both, (125 - 6 * k) % LANES, 1) for k in range(count)]


def tiles_of(planes):
    return [plane[8 * h : 8 * h + 8] for plane in planes for h in range(2)]


def own_rows(nx, mine, recv_a, send_b, recv_b, coef, to_owner, to_block, rows):
    me = lax.axis_index("gx")
    for j in range(nx):
        pl.when(me != j)(to_owner(0, j).wait_recv)
    quarter = lax.broadcasted_iota(jnp.int32, (nx, LANES), 1) // 32
    row6 = recv_a[pl.ds(6 * EACH, nx, stride=SLOT), :]
    turns = [row6] + [pltpu.roll(row6, 32 * k, 1) for k in (1, 2, 3)]

    def spread(which):
        odd = (quarter - which) & 1
        high = (quarter - which) & 2
        return jnp.where(
            high == 0,
            jnp.where(odd == 0, turns[0], turns[1]),
            jnp.where(odd == 0, turns[2], turns[3]),
        )

    t_uu, t_ug, t_gu = spread(0), spread(1), spread(2)
    coef[0] = t_uu
    coef[1] = t_ug
    coef[2] = t_gu
    coef[3] = (1.0 + t_ug * t_gu) / t_uu
    coef[4] = spread(3)

    def at_row(which, j):
        return jnp.broadcast_to(coef[which, pl.ds(j, 1), :], (3 * EACH, LANES))

    blocks = [[at_row(which, j) for which in range(4)] for j in range(nx)]
    one = jnp.ones((3 * EACH, LANES), jnp.float32)
    from_left = [(0.0 * one, one)]
    for j in range(nx):
        uu, ug, gu, gg = blocks[j]
        u, g = from_left[-1]
        from_left.append((uu * u + ug * g, gu * u + gg * g))
    from_right = [None] * nx + [(at_row(4, nx - 1), one)]
    for j in range(nx - 1, -1, -1):
        uu, ug, gu, gg = blocks[j]
        u, h = from_right[j + 1]
        from_right[j] = (gg * u + ug * h, gu * u + uu * h)
    norm = -1.0 / from_right[0][0]
    left_sums, right_terms = [0.0 * one], []
    for j in range(nx):
        u_r = recv_a[pl.ds(SLOT * j, 3 * EACH), :]
        g_r = recv_a[pl.ds(SLOT * j + 3 * EACH, 3 * EACH), :]
        u, g = from_left[j + 1]
        left_sums.append(left_sums[-1] + (u * g_r - g * u_r))
        u, h = from_right[j + 1]
        right_terms.append(u * g_r + h * u_r)
    right_sum = 0.0 * one
    for d in range(nx - 1, -1, -1):
        right_sum = right_sum + right_terms[d]
        right, left = right_sum * norm, left_sums[d] * norm
        send_b[pl.ds(SLOT * d, 3 * EACH), :] = right * from_left[d][0] + left * from_right[d][0]
        send_b[pl.ds(SLOT * d + 3 * EACH, 3 * EACH), :] = right * from_left[d][1] - left * from_right[d][1]
    for d in B_ORDER:
        pl.when(me != d)(to_block(mine, d).start)

        @pl.when(me == d)
        def _():
            recv_b[rows(mine, 6 * EACH), :] = send_b[rows(d, 6 * EACH), :]


def solve_kernel(
    counts,
    density,
    momentum,
    face,
    local_out,
    phi_out,
    ends_out,
    face_s,
    state,
    flux_y,
    flux_zz,
    reduced_y,
    z_pack,
    z_left,
    z_right,
    send_a,
    recv_a,
    send_b,
    recv_b,
    coef,
    matrix_s,
    local,
    phi,
    in_sem,
    halo_send,
    halo_recv,
    a_send,
    a_recv,
    b_send,
    b_recv,
    out_sem,
    far_sem,
):
    nx, ny, nz = counts
    cells = state.shape[1]
    me = lax.axis_index("gx")

    barrier = pltpu.get_barrier_semaphore()
    near = [("gx", nx, k) for step in range(NEAR, 0, -1) for k in (step, -step)]
    near += [("gy", ny, 1), ("gy", ny, -1), ("gz", nz, 1), ("gz", nz, -1)]
    for axis, count, offset in near:
        pl.semaphore_signal(
            barrier, inc=1, device_id=neighbour(axis, count, offset), device_id_type=MESH
        )
    loads = [
        pltpu.make_async_copy(face, face_s, in_sem.at[0]),
        pltpu.make_async_copy(density, state.at[0], in_sem.at[1]),
        pltpu.make_async_copy(momentum.at[0], state.at[1], in_sem.at[2]),
        pltpu.make_async_copy(momentum.at[1], state.at[2], in_sem.at[3]),
    ]
    for load in loads:
        load.start()
    matrix_s[...] = stencil_matrix()
    for load in loads:
        load.wait()

    def inverse_face(i):
        return 1.0 / jnp.full((8, LANES), face_s[i], jnp.float32)

    def reduce_step(i, carry):
        pairs, base = carry
        inv = inverse_face(i)
        inv_rows = jnp.concatenate([inv, inv], 0)
        base = [(u + g * inv, g) for u, g in base]
        phi[0, i] = base[0][0]
        phi[1, i] = base[1][0]
        base = [(u, g + u) for u, g in base]
        rho, m0, m1 = state[0, i], state[1, i], state[2, i]
        over = 1.0 / rho
        speed_y = m0 * over
        speed_z = m1 * over
        yy, yz, zz = m0 * speed_y, m1 * speed_y, m1 * speed_z
        flux_y[0, i, 8:24] = m0
        flux_y[1, i, 8:24] = yy
        flux_y[2, i, 8:24] = yz
        flux_zz[i] = zz
        out = []
        for (u, g), value in zip(pairs, (rho, m0, m1, yy, yz, zz)):
            u = u + g * inv_rows
            out.append((u, g + (u - value)))
        return out, base

    def reduce_steps(block, carry):
        for k in range(4):
            carry = reduce_step(4 * block + k, carry)
        return carry

    zero = jnp.zeros((16, LANES), jnp.float32)
    unit = jnp.ones((8, LANES), jnp.float32)
    pairs, base = lax.fori_loop(
        0,
        cells // 4,
        reduce_steps,
        ([(zero, zero)] * 6, [(unit, 0.0 * unit), (0.0 * unit, unit)]),
    )
    rho_r, m0_r, m1_r, yy_r, yz_r, zz_r = pairs
    plain = [value for pair in (rho_r, m0_r, m1_r) for value in pair]
    by_y = [value for pair in (m0_r, yy_r, yz_r) for value in pair]
    by_z = [value for pair in (m1_r, yz_r, zz_r) for value in pair]
    for k in range(6):
        reduced_y[k, 8:24] = by_y[k]
    z_pack[cells // 2] = pack_lanes(tiles_of(by_z))

    pl.semaphore_wait(barrier, len(near))
    for offset in (NEAR, -NEAR):
        pl.semaphore_signal(
            far_sem, inc=1, device_id=neighbour("gx", nx, offset), device_id_type=MESH
        )

    def halo(which, source, target, axis, count, offset):
        return pltpu.make_async_remote_copy(
            source,
            target,
            halo_send.at[which],
            halo_recv.at[which],
            device_id=neighbour(axis, count, offset),
            device_id_type=MESH,
        )

    last = cells // 2
    near_halos = [
        halo(0, reduced_y.at[:, 21:24], reduced_y.at[:, 5:8], "gy", ny, 1),
        halo(1, reduced_y.at[:, 8:11], reduced_y.at[:, 24:27], "gy", ny, -1),
        halo(2, z_pack.at[last], z_left.at[last], "gz", nz, 1),
        halo(3, z_pack.at[last], z_right.at[last], "gz", nz, -1),
    ]
    for copy in near_halos:
        copy.start()
    raw_y = [
        halo(4, flux_y.at[:, :, 21:24], flux_y.at[:, :, 5:8], "gy", ny, 1),
        halo(5, flux_y.at[:, :, 8:11], flux_y.at[:, :, 24:27], "gy", ny, -1),
    ]
    for copy in raw_y:
        copy.start()

    (u1, g1), (u2, g2) = base
    quarter = lax.broadcasted_iota(jnp.int32, (8, LANES), 1) // 32
    row6 = jnp.where(
        quarter < 2,
        jnp.where(quarter == 0, u1, u2),
        jnp.where(quarter == 2, g1, inverse_face(cells - 1)),
    )
    send_a[pl.ds(6 * EACH, OWNERS, stride=SLOT), :] = jnp.concatenate([row6] * (OWNERS // 8), 0)

    def pack_step(p, _):
        planes = []
        for q in range(2):
            i = 2 * p + q
            planes += [state[2, i], flux_y[2, i, 8:24], flux_zz[i]]
        z_pack[p] = pack_lanes(tiles_of(planes))
        return _

    lax.fori_loop(0, last, pack_step, 0)
    raw_z = [
        halo(6, z_pack.at[0:last], z_left.at[0:last], "gz", nz, 1),
        halo(7, z_pack.at[0:last], z_right.at[0:last], "gz", nz, -1),
    ]
    for copy in raw_z:
        copy.start()

    for copy in near_halos:
        copy.wait_recv()
    own_z = jnp.concatenate(by_z, 0)
    halo_z = jnp.concatenate(unpack_lanes(z_left[last], z_right[last], 12), 0)
    diff_z = along_z(own_z, halo_z, matrix_s[...])
    for f in range(3):
        for v in range(2):
            k = 2 * f + v
            diff_y = along_y(lambda step: reduced_y[k, pl.ds(8 + step, 16), :])
            value = plain[k] - SCALE * (diff_y + diff_z[16 * k : 16 * k + 16])
            for r in range(EACH):
                at = EACH * (3 * v + f) + r
                part = value[OWNERS * r : OWNERS * (r + 1)]
                send_a[pl.ds(at, OWNERS, stride=SLOT), :] = part

    def rows(index, count):
        return pl.ds(pl.multiple_of(index * SLOT, 8), count)

    owners = OWNER_LIST
    mine = sum(c * (me == owner).astype(jnp.int32) for c, owner in enumerate(owners))
    is_owner = functools.reduce(jnp.logical_or, [me == owner for owner in owners])

    def to_owner(c, source):
        return pltpu.make_async_remote_copy(
            send_a.at[rows(c, 6 * EACH + 1)],
            recv_a.at[rows(source, 6 * EACH + 1)],
            a_send.at[c],
            a_recv.at[source],
            device_id={"gx": owners[c]},
            device_id_type=MESH,
        )

    def to_block(c, target):
        return pltpu.make_async_remote_copy(
            send_b.at[rows(target, 6 * EACH)],
            recv_b.at[rows(c, 6 * EACH)],
            b_send.at[target],
            b_recv.at[c],
            device_id={"gx": target},
            device_id_type=MESH,
        )

    pl.semaphore_wait(far_sem, 2)
    def hand_over(c, going):
        pl.when(going & (me != owners[c]))(to_owner(c, me).start)

        @pl.when(going & (me == owners[c]))
        def _():
            recv_a[rows(me, 6 * EACH + 1), :] = send_a[rows(c, 6 * EACH + 1), :]

    for c in LATE_OWNERS:
        hand_over(c, me < nx // 2)
    for c in EARLY_OWNERS:
        hand_over(c, me >= 0)
    for c in LATE_OWNERS:
        hand_over(c, me >= nx // 2)

    for copy in raw_y + raw_z:
        copy.wait_recv()

    def local_step(p, carry):
        planes = []
        for q in range(2):
            i = 2 * p + q
            planes += [state[2, i], flux_y[2, i, 8:24], flux_zz[i]]
        halos = unpack_lanes(z_left[p], z_right[p], 12)
        diff_z = along_z(jnp.concatenate(planes, 0), jnp.concatenate(halos, 0), matrix_s[...])
        for q in range(2):
            i = 2 * p + q
            inv = inverse_face(i)
            inv_rows = jnp.concatenate([inv, inv], 0)
            new = []
            for f, (u, g) in enumerate(carry):
                diff_y = along_y(lambda step: flux_y[f, i, pl.ds(8 + step, 16), :])
                at = 16 * (3 * q + f)
                value = state[f, i] - SCALE * (diff_y + diff_z[at : at + 16])
                u = u + g * inv_rows
                local[f, i] = u
                new.append((u, g + (u - value)))
            carry = new
        return carry

    lax.fori_loop(0, last, local_step, [(zero, zero)] * 3)
    stores = [
        pltpu.make_async_copy(local, local_out, out_sem.at[0]),
        pltpu.make_async_copy(phi, phi_out, out_sem.at[1]),
    ]
    for store in stores:
        store.start()

    @pl.when(is_owner)
    def _():
        own_rows(nx, mine, recv_a, send_b, recv_b, coef, to_owner, to_block, rows)

    for copy in near_halos + raw_y + raw_z:
        copy.wait_send()
    for store in stores:
        store.wait()
    for c in range(OWNERS):
        pl.when(me != owners[c])(to_block(c, me).wait_recv)
    for v in range(2):
        for f in range(3):
            for r in range(EACH):
                at = EACH * (3 * v + f) + r
                part = recv_b[pl.ds(at, OWNERS, stride=SLOT), :]
                ends_out[v, f, OWNERS * r : OWNERS * (r + 1)] = part
    for c in range(OWNERS):
        pl.when(me != owners[c])(to_owner(c, me).wait_send)
    for d in range(nx):
        pl.when(is_owner & (me != d))(to_block(mine, d).wait_send)


def combine_kernel(local, phi, ends, out, staged, sems):
    starts = [(ends[0, f], ends[1, f]) for f in range(3)]
    cells = local.shape[1]
    size = cells // PARTS
    stores = []
    for part in range(PARTS):
        span = pl.ds(part * size, size)
        for i in range(part * size, (part + 1) * size):
            by_u = jnp.concatenate([phi[0, i]] * 2, 0)
            by_g = jnp.concatenate([phi[1, i]] * 2, 0)
            for f, (u, g) in enumerate(starts):
                staged[f, i] = local[f, i] + (by_u * u + by_g * g)
        store = pltpu.make_async_copy(staged.at[:, span], out.at[:, span], sems.at[part])
        store.start()
        stores.append(store)
    for store in stores:
        store.wait()


def on_device(density, momentum, lower_face):
    counts = tuple(lax.axis_size(axis) for axis in ("gx", "gy", "gz"))
    nx = counts[0]
    cells, rows, lanes = density.shape
    block = (3, cells, rows, lanes)
    f32 = jnp.float32
    sems = pltpu.SemaphoreType.DMA
    local, phi, ends = pl.pallas_call(
        functools.partial(solve_kernel, counts),
        out_shape=(
            jax.ShapeDtypeStruct(block, f32),
            jax.ShapeDtypeStruct((2, cells, 8, lanes), f32),
            jax.ShapeDtypeStruct((2, 3, rows, lanes), f32),
        ),
        in_specs=[HBM, HBM, HBM],
        out_specs=(ANY, ANY, VMEM),
        scratch_shapes=[
            pltpu.SMEM((cells,), f32),
            pltpu.VMEM(block, f32),
            pltpu.VMEM((3, cells, 32, lanes), f32),
            pltpu.VMEM((cells, rows, lanes), f32),
            pltpu.VMEM((6, 32, lanes), f32),
            pltpu.VMEM((cells // 2 + 1, 8, lanes), f32),
            pltpu.VMEM((cells // 2 + 1, 8, lanes), f32),
            pltpu.VMEM((cells // 2 + 1, 8, lanes), f32),
            pltpu.VMEM((OWNERS * SLOT, lanes), f32),
            pltpu.VMEM((nx * SLOT, lanes), f32),
            pltpu.VMEM((nx * SLOT, lanes), f32),
            pltpu.VMEM((OWNERS * SLOT, lanes), f32),
            pltpu.VMEM((5, nx, lanes), f32),
            pltpu.VMEM((2 * lanes, lanes), jnp.bfloat16),
            pltpu.VMEM(block, f32),
            pltpu.VMEM((2, cells, 8, lanes), f32),
            sems((4,)),
            sems((8,)),
            sems((8,)),
            sems((nx,)),
            sems((nx,)),
            sems((nx,)),
            sems((nx,)),
            sems((2,)),
            pltpu.SemaphoreType.REGULAR,
        ],
        compiler_params=pltpu.CompilerParams(
            collective_id=0, has_side_effects=True, vmem_limit_bytes=16 << 20
        ),
        name="solve",
    )(*(pltpu.with_memory_space_constraint(x, pltpu.HBM) for x in (density, momentum, lower_face)))
    return pl.pallas_call(
        combine_kernel,
        out_shape=jax.ShapeDtypeStruct(block, f32),
        in_specs=[VMEM, VMEM, VMEM],
        out_specs=ANY,
        scratch_shapes=[pltpu.VMEM(block, f32), sems((PARTS,))],
        compiler_params=pltpu.CompilerParams(vmem_limit_bytes=16 << 20),
        name="combine",
    )(local, phi, ends)


def solution(mesh):
    placed = (P("gx", "gy", "gz"), P(None, "gx", "gy", "gz"), P("gx"))
    return jax.shard_map(
        on_device, mesh=mesh, in_specs=placed, out_specs=P(None, "gx", "gy", "gz"), check_vma=False
    )
```
